32 devices in a mesh: lat: 4 (over y, x), lon: 8 (over z, core).
Axes of the slice: x: 2, y: 2, z: 4, core: 2. Of those that a mesh axis runs over, the one named last changes fastest.
Arguments:
- fields: bfloat16 [192, 256, 2, 256], P('lat', 'lon'), may hold values from -6 to 6
- ocean_mask: int32 [24, 32], P('lat'), may hold values from 0 to 1, as said below
- gain_one: float32 [256], replicated, may hold values from 0.1 to 1.9
- w_qkv: bfloat16 [256, 768], replicated, may hold values from -0.375 to 0.375
- rel_bias: float32 [8, 675], replicated, may hold values from -80 to 150
- w_proj: bfloat16 [256, 256], replicated, may hold values from -0.375 to 0.375
- gain_two: float32 [256], replicated, may hold values from 0.1 to 1.9
- w_up: bfloat16 [256, 1024], replicated, may hold values from -0.375 to 0.375
- w_down: bfloat16 [1024, 256], replicated, may hold values from -0.1875 to 0.1875
Outputs:
- ocean_out: bfloat16 [192, 256, 2, 256], P('lat', 'lon')
The draws below stay inside these ranges and needn't reach their ends.
Inputs may be any that keep to these rules, and one draw needn't show every extreme that they name: `ocean_mask`: the windows of the last row of windows (a = 23) are land. Each band of 6 rows of windows held by one index of lat holds exactly 10 ocean windows per longitude device. Taking the devices of a band in order of longitude index, each holding 4 columns of windows, the ocean windows of the first d devices number at least d * 10 and at most d * 10 + 10; the upper bound is reached for some d in every band, at places drawn anew. One device holds 0 to 20 ocean windows.
All inputs are finite; a program needn't handle non-finite values.
Results may differ from the reference program's by a relative error of at most 0.0057.
Values may be sent and summed in bfloat16 or wider, within the bound.
A program may use at most 64 MiB of HBM per device.

```python
import math
import jax
import jax.numpy as jnp
from jax import lax

C = 256
HEADS = 8
FF = 1024
WIN_LAT = 8
WIN_LON = 8
DEPTH = 2
LAT_WIN = 6
LON_WIN = 4
SLOTS = 10
BIAS_LEN = 675
NLAT_WIN = 24
NLON_WIN = 32
NLAT = 192
NLON = 256
OCEAN = 320
N_LAT = 4
N_LON = 8


def band_mask(key, band):
    first_key, second_key, third_key = jax.random.split(key, 3)
    device_ids = jnp.arange(N_LON, dtype=jnp.int32)
    excess = jax.random.randint(first_key, (N_LON,), 0, SLOTS + 1, dtype=jnp.int32)
    spot = jax.random.randint(second_key, (), 0, N_LON - 1, dtype=jnp.int32)
    excess = jnp.where(device_ids == spot, SLOTS, excess)
    excess = jnp.where(device_ids == spot - 1, 0, excess)
    excess = jnp.where(device_ids == N_LON - 1, 0, excess)
    earlier = jnp.concatenate([jnp.zeros((1,), jnp.int32), excess[:-1]])
    counts = SLOTS + excess - earlier
    total_windows = LAT_WIN * LON_WIN
    window_rows = jnp.arange(total_windows, dtype=jnp.int32) // LON_WIN
    blocked = jnp.logical_and(band == N_LAT - 1, window_rows == LAT_WIN - 1).astype(jnp.int32)

    def one_device(device, count):
        shuffled = jax.random.permutation(jax.random.fold_in(third_key, device), total_windows).astype(jnp.int32)
        score_ids = shuffled + total_windows * blocked
        ranking = jnp.argsort(jnp.argsort(score_ids))
        return (ranking < count).astype(jnp.int32).reshape(LAT_WIN, LON_WIN)
    tiles = jax.vmap(one_device)(device_ids, counts)
    return tiles.transpose(1, 0, 2).reshape(LAT_WIN, N_LON * LON_WIN)


def draw_ocean_mask(key, part):
    band_ids = jnp.arange(N_LAT, dtype=jnp.int32)
    keyed = jax.vmap(lambda band_id: jax.random.fold_in(key, band_id))(band_ids)
    bands = jax.vmap(band_mask)(keyed, band_ids)
    return bands.reshape(NLAT_WIN, NLON_WIN)


def draw_rel_bias(key, part):
    first_key, second_key, third_key = jax.random.split(jax.random.fold_in(key, 17), 3)
    table = jax.random.uniform(first_key, (HEADS, BIAS_LEN), jnp.float32, -2.0, 2.0)
    return table


def shard_levels(key, shape, shards, low, largest):
    gain = 1.0
    for dim, parts in shards:
        draws = jax.random.uniform(jax.random.fold_in(jax.random.fold_in(key, 6), dim), (parts,), jnp.float32, low / len(shards), largest / len(shards))
        gain = gain * jnp.repeat(jnp.exp(draws), shape[dim] // parts).reshape((-1,) + (1,) * (len(shape) - 1 - dim))
    return gain


def noise(key, shape, deviation, most, cuts=(), kind=jnp.bfloat16):
    array = deviation * jax.random.normal(key, shape, jnp.float32)
    if cuts:
        array = array * shard_levels(key, shape, cuts, -0.22, 0.18)
    return jnp.clip(array, -most, most).astype(kind)


def setup_inputs(seed: int = 0) -> dict:
    seeds = jax.random.split(jax.random.key(seed), 10)
    return {
        "fields": noise(seeds[0], (NLAT, NLON, DEPTH, C), 1.0, 6.0, ((0, 4), (1, 8))),
        "ocean_mask": draw_ocean_mask(jax.random.fold_in(seeds[9], 71), 0),
        "gain_one": jnp.clip(1.0 + 0.18 * jax.random.normal(seeds[2], (C,), jnp.float32), 0.1, 1.9),
        "w_qkv": noise(seeds[3], (C, 3 * C), C ** -0.5, 0.375),
        "rel_bias": draw_rel_bias(jax.random.fold_in(seeds[9], 71), 0),
        "w_proj": noise(seeds[5], (C, C), C ** -0.5, 0.375),
        "gain_two": jnp.clip(1.0 + 0.18 * jax.random.normal(seeds[6], (C,), jnp.float32), 0.1, 1.9),
        "w_up": noise(seeds[7], (C, FF), C ** -0.5, 0.375),
        "w_down": noise(seeds[8], (FF, C), FF ** -0.5, 0.1875),
    }


NORM_FLOOR = 0.25

def product(form, left, right):
    return jnp.einsum(form, left.astype(jnp.float32), right.astype(jnp.float32), precision=lax.Precision.HIGHEST)

def layer_norm(values, gain_vec):
    average = lax.optimization_barrier(jnp.mean(values, axis=-1, keepdims=True))
    centred = values - average
    spread = lax.optimization_barrier(jnp.mean(centred * centred, axis=-1, keepdims=True))
    return centred / jnp.sqrt(spread + NORM_FLOOR) * gain_vec

def bias_table(rel_bias, win_lat, win_lon, levels):
    tokens = win_lat * win_lon * levels
    token_ids = jnp.arange(tokens, dtype=jnp.int32)
    token_row = token_ids // (win_lon * levels)
    token_col = token_ids // levels % win_lon
    token_lev = token_ids % levels
    row_gap = token_row[:, None] - token_row[None, :] + win_lat - 1
    col_gap = token_col[:, None] - token_col[None, :] + win_lon - 1
    lev_gap = token_lev[:, None] - token_lev[None, :] + levels - 1
    lookup = ((row_gap * (2 * win_lon - 1) + col_gap) * (2 * levels - 1) + lev_gap).astype(jnp.int32)
    return jnp.take(rel_bias, lookup, axis=1)

def window_block(block, weights):
    gain_one, w_qkv, bias_full, w_proj, gain_two, w_up, w_down = weights
    window_count, tokens, features = block.shape
    head_count = bias_full.shape[0]
    head_dim = features // head_count
    score_scale = 1.0 / math.sqrt(head_dim)
    normed = layer_norm(block.astype(jnp.float32), gain_one).astype(jnp.bfloat16)
    triple = product('ntc,cf->ntf', normed, w_qkv).astype(jnp.bfloat16)
    triple = triple.reshape(window_count, tokens, 3, head_count, head_dim)
    query_part = triple[:, :, 0]
    key_part = triple[:, :, 1]
    value_part = triple[:, :, 2]
    scores = product('nthd,nshd->nhts', query_part, key_part) * score_scale + bias_full[None]
    row_top = lax.optimization_barrier(jnp.max(scores, axis=-1, keepdims=True))
    exponent = jnp.exp(scores - row_top)
    attn_prob = (exponent / lax.optimization_barrier(jnp.sum(exponent, axis=-1, keepdims=True))).astype(jnp.bfloat16)
    mixed = product('nhts,nshd->nthd', attn_prob, value_part).astype(jnp.bfloat16)
    mixed = mixed.reshape(window_count, tokens, features)
    middle = (block.astype(jnp.float32) + product('ntc,cf->ntf', mixed, w_proj)).astype(jnp.bfloat16)
    normed_two = layer_norm(middle.astype(jnp.float32), gain_two).astype(jnp.bfloat16)
    hidden = jax.nn.gelu(product('ntc,cf->ntf', normed_two, w_up), approximate=False).astype(jnp.bfloat16)
    return (middle.astype(jnp.float32) + product('ntf,fc->ntc', hidden, w_down)).astype(jnp.bfloat16)

def run_windows(windows, weights):
    total_rows = windows.shape[0]
    block_size = 8 if total_rows % 8 == 0 else total_rows
    grouped = windows.reshape((total_rows // block_size, block_size) + windows.shape[1:])

    def one_group(group_win):
        return window_block(group_win, weights)
    finished = lax.map(one_group, grouped)
    return finished.reshape(windows.shape)

def reference(fields, ocean_mask, gain_one, w_qkv, rel_bias, w_proj, gain_two, w_up, w_down):
    lat_cells, lon_cells, levels, features = fields.shape
    lat_half = WIN_LAT // 2
    lon_half = WIN_LON // 2
    shifted = jnp.concatenate([fields[lat_half:], jnp.zeros_like(fields[:lat_half])], axis=0)
    shifted = jnp.roll(shifted, -lon_half, axis=1)
    lat_windows = lat_cells // WIN_LAT
    lon_windows = lon_cells // WIN_LON
    total_windows = lat_windows * lon_windows
    windows = shifted.reshape(lat_windows, WIN_LAT, lon_windows, WIN_LON, levels, features)
    windows = windows.transpose(0, 2, 1, 3, 4, 5).reshape(total_windows, WIN_LAT * WIN_LON * levels, features)
    flat_mask = ocean_mask.reshape(total_windows).astype(jnp.int32)
    window_ids = jnp.arange(total_windows, dtype=jnp.int32)
    ocean_order = jnp.argsort((1 - flat_mask) * total_windows + window_ids)[:OCEAN].astype(jnp.int32)
    picked = jnp.take(windows, ocean_order, axis=0)
    bias_full = bias_table(rel_bias, WIN_LAT, WIN_LON, levels)
    weights = (gain_one, w_qkv, bias_full, w_proj, gain_two, w_up, w_down)
    finished = run_windows(picked, weights)
    result = jnp.zeros_like(windows).at[ocean_order].set(finished)
    result = result.reshape(lat_windows, lon_windows, WIN_LAT, WIN_LON, levels, features)
    return result.transpose(0, 2, 1, 3, 4, 5).reshape(lat_cells, lon_cells, levels, features)
```

```python
import functools
import math

import jax
import jax.numpy as jnp
from jax import lax
from jax.experimental import pallas as pl
from jax.experimental.pallas import tpu as pltpu
from jax.sharding import PartitionSpec as P

WIN_LAT = 8
WIN_LON = 8
NORM_FLOOR = 0.25
LOG2E = math.log2(math.e)
ERF_COEFS = (1.1283793294596702, 0.10276689183983656, -0.0001854270054620651, -0.000625856981717449, 9.00024455627471e-05, -6.058558938836915e-06, 1.6416008301278458e-07)
ERF_LIMIT = 15.209999999999999


def bias_strips(rel_bias, levels):
    heads, length = rel_bias.shape
    col_step = 2 * levels - 1
    row_step = (2 * WIN_LON - 1) * col_step
    offsets = [c * col_step + lev for c in range(WIN_LON) for lev in range(levels)]
    top = offsets[-1]
    width = length - top
    scaled = rel_bias * LOG2E
    left = jnp.stack([scaled[:, top - q : top - q + width] for q in offsets], axis=1)
    group = WIN_LON * levels
    lane = jnp.arange(2 * WIN_LAT * group, dtype=jnp.int32)
    inner = lane % group
    target = lane // group * row_step + inner // levels * col_step + inner % levels
    pick = jnp.arange(width, dtype=jnp.int32)[:, None] == target[None, :]
    strips = jnp.dot(
        left.reshape(heads * group, width),
        pick.astype(jnp.float32),
        precision=lax.Precision.HIGHEST,
    )
    return strips.reshape(heads, group, 2 * WIN_LAT * group)


def gather_kernel(
    slots, half, mask_ref, where_ref, fields, north, east, corner, own, out_late, out_early, info, sems
):
    lat_windows = mask_ref.shape[0]
    lon_windows = fields.shape[1] // WIN_LON
    lat_half, lon_half = WIN_LAT // 2, WIN_LON // 2
    index = where_ref[0]
    first_col = index * lon_windows

    def count(col, total):
        for row in range(lat_windows):
            total = total + mask_ref[row, col]
        return total

    before = lax.fori_loop(0, first_col, count, jnp.int32(0))
    owned = lax.fori_loop(first_col, first_col + lon_windows, count, jnp.int32(0))
    kept = slots - (before - index * slots)
    to_east = before + owned - (index + 1) * slots
    info[0] = kept
    info[1] = slots - to_east - kept

    def fetch(row, col, window, block):
        low_lat, low_lon = row * WIN_LAT + lat_half, col * WIN_LON + lon_half
        last_row, last_col = row == lat_windows - 1, col == lon_windows - 1

        def quarter(source, down, right):
            target = block.at[pl.ds(down, lat_half), pl.ds(right, lon_half)]
            pltpu.make_async_copy(source, target, sems.at[window]).start()

        here = (pl.ds(low_lat, lat_half), pl.ds(low_lon, lon_half))
        quarter(fields.at[here[0], here[1]], 0, 0)

        @pl.when(jnp.logical_not(last_col))
        def _():
            quarter(fields.at[here[0], pl.ds(low_lon + lon_half, lon_half)], 0, lon_half)

        @pl.when(last_col)
        def _():
            quarter(east.at[here[0]], 0, lon_half)

        @pl.when(jnp.logical_not(last_row))
        def _():
            below = pl.ds(low_lat + lat_half, lat_half)
            quarter(fields.at[below, here[1]], lat_half, 0)

            @pl.when(jnp.logical_not(last_col))
            def _():
                quarter(fields.at[below, pl.ds(low_lon + lon_half, lon_half)], lat_half, lon_half)

            @pl.when(last_col)
            def _():
                quarter(east.at[below], lat_half, lon_half)

        @pl.when(last_row)
        def _():
            quarter(north.at[:, here[1]], lat_half, 0)

            @pl.when(jnp.logical_not(last_col))
            def _():
                quarter(north.at[:, pl.ds(low_lon + lon_half, lon_half)], lat_half, lon_half)

            @pl.when(last_col)
            def _():
                quarter(corner, lat_half, lon_half)

    def start(window, rank):
        row, col = window // lon_windows, window % lon_windows
        ocean = mask_ref[row, first_col + col]
        slot = slots - to_east + rank - kept

        @pl.when((ocean == 1) & (rank < kept))
        def _():
            fetch(row, col, window, own.at[rank])

        @pl.when((ocean == 1) & (rank >= kept) & (slot >= half))
        def _():
            fetch(row, col, window, out_late.at[slot - half])

        @pl.when((ocean == 1) & (rank >= kept) & (slot < half))
        def _():
            fetch(row, col, window, out_early.at[slot])

        return rank + ocean

    lax.fori_loop(0, lat_windows * lon_windows, start, jnp.int32(0))

    def finish(window, carry):
        row, col = window // lon_windows, window % lon_windows

        @pl.when(mask_ref[row, first_col + col] == 1)
        def _():
            block = fields.at[pl.ds(0, WIN_LAT), pl.ds(0, WIN_LON)]
            pltpu.make_async_copy(block, own.at[0], sems.at[window]).wait()

        return carry

    lax.fori_loop(0, lat_windows * lon_windows, finish, jnp.int32(0))


def place_kernel(
    half, mask_ref, where_ref, info, fin_early, fin_late, ret_early, ret_late, result, zero, sems
):
    lat_windows = mask_ref.shape[0]
    lon_windows = result.shape[1] // WIN_LON
    first_col = where_ref[0] * lon_windows
    zero[...] = jnp.zeros_like(zero)
    kept, ahead = info[0], info[1]

    def spot(window):
        row, col = window // lon_windows, window % lon_windows
        return result.at[pl.ds(row * WIN_LAT, WIN_LAT), pl.ds(col * WIN_LON, WIN_LON)]

    def start(window, rank):
        ocean = mask_ref[window // lon_windows, first_col + window % lon_windows]
        mine = rank < kept
        slot = jnp.where(mine, rank, rank + ahead)
        for pool, base, wanted, low in (
            (fin_early, 0, True, True),
            (fin_late, half, True, False),
            (ret_early, 0, False, True),
            (ret_late, half, False, False),
        ):
            side = mine if wanted else jnp.logical_not(mine)
            part = slot < half if low else slot >= half

            @pl.when((ocean == 1) & side & part)
            def _(pool=pool, base=base):
                pltpu.make_async_copy(
                    pool.at[slot - base], spot(window), sems.at[window]
                ).start()

        @pl.when(ocean == 0)
        def _():
            pltpu.make_async_copy(zero, spot(window), sems.at[window]).start()

        return rank + ocean

    lax.fori_loop(0, lat_windows * lon_windows, start, jnp.int32(0))

    def finish(window, carry):
        pltpu.make_async_copy(zero, spot(window), sems.at[window]).wait()
        return carry

    lax.fori_loop(0, lat_windows * lon_windows, finish, jnp.int32(0))


def normalise(values, gain):
    average = jnp.mean(values, axis=-1, keepdims=True)
    centred = values - average
    spread = jnp.mean(centred * centred, axis=-1, keepdims=True)
    return (centred * lax.rsqrt(spread + NORM_FLOOR) * gain).astype(jnp.bfloat16)


def erf_of(x):
    square = jnp.minimum(x * x, ERF_LIMIT)
    poly = jnp.full_like(square, ERF_COEFS[-1])
    for coef in ERF_COEFS[-2::-1]:
        poly = poly * square + coef
    return jnp.tanh(x * poly)


def dot(left, right):
    return jnp.dot(left, right, preferred_element_type=jnp.float32)


def window_kernel(
    base, info, own, arrived, strips, gain_one, w_qkv, w_proj, gain_two, w_up, w_down,
    out, bias, block, qkv, mixed,
):
    count = arrived.shape[0]
    heads, group, _ = strips.shape
    features = own.shape[-1]
    tokens = WIN_LAT * group
    dim = features // heads
    kept = info[0]
    scale = LOG2E / math.sqrt(dim)
    for row in range(WIN_LAT):
        first = (WIN_LAT - 1 - row) * group
        bias[:, row * group : (row + 1) * group, :] = strips[:, :, first : first + tokens]

    for n in range(count):
        slot = base + n

        @pl.when(slot < kept)
        def _():
            block[n * tokens : (n + 1) * tokens, :] = own[slot].reshape(tokens, features)

        @pl.when(slot >= kept)
        def _():
            block[n * tokens : (n + 1) * tokens, :] = arrived[n].reshape(tokens, features)

    values = block[...].astype(jnp.float32)
    normed = normalise(values, gain_one[...])
    qkv[...] = dot(normed, w_qkv[...]).astype(jnp.bfloat16)
    lane_head = lax.broadcasted_iota(jnp.int32, (tokens, features), 1) // dim

    def attend(n, carry):
        rows = pl.ds(pl.multiple_of(n * tokens, tokens), tokens)
        query_t = qkv[rows, :features].T
        key = qkv[rows, features : 2 * features]
        value_t = qkv[rows, 2 * features :].T
        parts = []
        for h in range(heads):
            masked = jnp.where(lane_head == h, key, jnp.zeros_like(key))
            scores = dot(masked, query_t) * scale + bias[h]
            power = jnp.exp2(scores - jnp.max(scores, axis=0, keepdims=True))
            total = jnp.sum(power, axis=0, keepdims=True)
            part = dot(value_t[h * dim : (h + 1) * dim, :], power.astype(jnp.bfloat16))
            parts.append((part * (1.0 / total)).astype(jnp.bfloat16))
        mixed[rows, :] = jnp.concatenate(parts, axis=0).T
        return carry

    lax.fori_loop(0, count, attend, 0, unroll=True)
    middle = (values + dot(mixed[...], w_proj[...])).astype(jnp.bfloat16)
    middle_wide = middle.astype(jnp.float32)
    normed_two = normalise(middle_wide, gain_two[...])
    total = middle_wide
    step = 256
    for k in range(w_up.shape[1] // step):
        cols = slice(k * step, (k + 1) * step)
        up = dot(normed_two, w_up[:, cols])
        grown = (0.5 * up * (1.0 + erf_of(up * math.sqrt(0.5)))).astype(jnp.bfloat16)
        total = total + dot(grown, w_down[cols, :])
    out[...] = total.astype(jnp.bfloat16).reshape(out.shape)


def vmem():
    return pl.BlockSpec(memory_space=pltpu.VMEM)


def smem():
    return pl.BlockSpec(memory_space=pltpu.SMEM)


def any_space():
    return pl.BlockSpec(memory_space=pl.ANY)


def cost(flops, moved):
    return pl.CostEstimate(flops=flops, bytes_accessed=moved, transcendentals=0)


def run_windows(base, info, own, arrived, strips, gain_one, w_qkv, w_proj, gain_two, w_up, w_down):
    count, _, _, levels, features = arrived.shape
    heads = strips.shape[0]
    tokens = WIN_LAT * WIN_LON * levels
    flops = 2 * count * tokens * features * (
        w_qkv.shape[1] + w_proj.shape[1] + 2 * w_up.shape[1] + 4 * tokens
    )
    return pl.pallas_call(
        functools.partial(window_kernel, base),
        out_shape=jax.ShapeDtypeStruct(arrived.shape, arrived.dtype),
        in_specs=[smem()] + [vmem()] * 9,
        out_specs=vmem(),
        scratch_shapes=[
            pltpu.VMEM((heads, tokens, tokens), jnp.float32),
            pltpu.VMEM((count * tokens, features), jnp.bfloat16),
            pltpu.VMEM((count * tokens, 3 * features), jnp.bfloat16),
            pltpu.VMEM((count * tokens, features), jnp.bfloat16),
        ],
        cost_estimate=cost(flops, 4 * arrived.size),
        compiler_params=pltpu.CompilerParams(vmem_limit_bytes=48 * 2**20),
    )(info, own, arrived, strips, gain_one, w_qkv, w_proj, gain_two, w_up, w_down)


def body(fields, ocean_mask, gain_one, w_qkv, rel_bias, w_proj, gain_two, w_up, w_down):
    lat_cells, lon_cells, levels, features = fields.shape
    lat_windows = lat_cells // WIN_LAT
    lon_windows = lon_cells // WIN_LON
    slots = (lat_windows - 1) * lon_windows // 2
    half = slots // 2
    late = slots - half
    lat_half, lon_half = WIN_LAT // 2, WIN_LON // 2
    lat_size, lon_size = lax.axis_size("lat"), lax.axis_size("lon")
    south = [(i, i - 1) for i in range(1, lat_size)]
    west = [(i, (i - 1) % lon_size) for i in range(lon_size)]
    diagonal = [
        (i * lon_size + j, (i - 1) * lon_size + (j - 1) % lon_size)
        for i in range(1, lat_size)
        for j in range(lon_size)
    ]
    onward = [(i, i + 1) for i in range(lon_size - 1)]
    backward = [(i + 1, i) for i in range(lon_size - 1)]
    east = lax.ppermute(fields[:, :lon_half], "lon", west)
    north = lax.ppermute(fields[:lat_half], "lat", south)
    corner = lax.ppermute(fields[:lat_half, :lon_half], ("lat", "lon"), diagonal)
    strips = bias_strips(rel_bias, levels)
    where = jnp.reshape(lax.axis_index("lon"), (1,)).astype(jnp.int32)
    shape = (WIN_LAT, WIN_LON, levels, features)
    window_count = lat_windows * lon_windows
    own, out_late, out_early, info = pl.pallas_call(
        functools.partial(gather_kernel, slots, half),
        out_shape=[
            jax.ShapeDtypeStruct((slots,) + shape, fields.dtype),
            jax.ShapeDtypeStruct((late,) + shape, fields.dtype),
            jax.ShapeDtypeStruct((half,) + shape, fields.dtype),
            jax.ShapeDtypeStruct((2,), jnp.int32),
        ],
        in_specs=[smem(), smem()] + [any_space()] * 4,
        out_specs=[vmem(), vmem(), vmem(), smem()],
        scratch_shapes=[pltpu.SemaphoreType.DMA((window_count,))],
        cost_estimate=cost(0, 4 * fields.size),
    )(ocean_mask, where, fields, north, east, corner)
    in_late = lax.ppermute(out_late, "lon", onward)
    in_early = lax.ppermute(out_early, "lon", onward)
    weights = (
        strips, gain_one.reshape(1, -1), w_qkv, w_proj, gain_two.reshape(1, -1), w_up, w_down,
    )
    fin_late = run_windows(half, info, own, in_late, *weights)
    ret_late = lax.ppermute(fin_late, "lon", backward)
    fin_early = run_windows(0, info, own, in_early, *weights)
    ret_early = lax.ppermute(fin_early, "lon", backward)
    return pl.pallas_call(
        functools.partial(place_kernel, half),
        out_shape=jax.ShapeDtypeStruct(fields.shape, fields.dtype),
        in_specs=[smem()] * 3 + [vmem()] * 4,
        out_specs=any_space(),
        scratch_shapes=[
            pltpu.VMEM(shape, fields.dtype),
            pltpu.SemaphoreType.DMA((window_count,)),
        ],
        cost_estimate=cost(0, 4 * fields.size),
    )(ocean_mask, where, info, fin_early, fin_late, ret_early, ret_late)


def solution(mesh):
    in_specs = (P("lat", "lon", None, None), P("lat", None), P(), P(), P(), P(), P(), P(), P())
    out_specs = P("lat", "lon", None, None)
    return jax.shard_map(body, mesh=mesh, in_specs=in_specs, out_specs=out_specs, check_vma=False)
```

```python
import functools
import math

import jax
import jax.numpy as jnp
from jax import lax
from jax.experimental import pallas as pl
from jax.experimental.pallas import tpu as pltpu
from jax.sharding import PartitionSpec as P

WIN_LAT = 8
WIN_LON = 8
NORM_FLOOR = 0.25
MESH = pl.DeviceIdType.MESH
LOG2E = math.log2(math.e)
ERF_COEFS = (1.1283793294596702, 0.10276689183983656, -0.0001854270054620651, -0.000625856981717449, 9.00024455627471e-05, -6.058558938836915e-06, 1.6416008301278458e-07)
ERF_LIMIT = 15.209999999999999


def bias_strips(rel_bias, levels):
    heads, length = rel_bias.shape
    col_step = 2 * levels - 1
    row_step = (2 * WIN_LON - 1) * col_step
    offsets = [c * col_step + lev for c in range(WIN_LON) for lev in range(levels)]
    top = offsets[-1]
    width = length - top
    scaled = rel_bias * LOG2E
    left = jnp.stack([scaled[:, top - q : top - q + width] for q in offsets], axis=1)
    group = WIN_LON * levels
    lane = jnp.arange(2 * WIN_LAT * group, dtype=jnp.int32)
    inner = lane % group
    target = lane // group * row_step + inner // levels * col_step + inner % levels
    pick = jnp.arange(width, dtype=jnp.int32)[:, None] == target[None, :]
    strips = jnp.dot(
        left.reshape(heads * group, width),
        pick.astype(jnp.float32),
        precision=lax.Precision.HIGHEST,
    )
    return strips.reshape(heads, group, 2 * WIN_LAT * group)


def halo_kernel(fields, north, east, corner, send_sems, recv_sems):
    lat_half, lon_half = WIN_LAT // 2, WIN_LON // 2
    lat, lon = lax.axis_index("lat"), lax.axis_index("lon")
    lat_size, lon_size = lax.axis_size("lat"), lax.axis_size("lon")
    west, east_of = (lon + lon_size - 1) % lon_size, (lon + 1) % lon_size
    barrier = pltpu.get_barrier_semaphore()

    def greet(row, col):
        pl.semaphore_signal(barrier, inc=1, device_id=(row, col), device_id_type=MESH)

    greet(lat, east_of)

    @pl.when(lat < lat_size - 1)
    def _():
        greet(lat + 1, lon)
        greet(lat + 1, east_of)

    def transfer(which, source, target, row, col):
        return pltpu.make_async_remote_copy(
            src_ref=source,
            dst_ref=target,
            send_sem=send_sems.at[which],
            recv_sem=recv_sems.at[which],
            device_id=(row, col),
            device_id_type=MESH,
        )

    up = jnp.maximum(lat - 1, 0)
    to_west = transfer(0, fields.at[:, pl.ds(0, lon_half)], east, lat, west)
    to_north = transfer(1, fields.at[pl.ds(0, lat_half)], north, up, lon)
    to_corner = transfer(
        2, fields.at[pl.ds(0, lat_half), pl.ds(0, lon_half)], corner, up, west
    )

    @pl.when(lat > 0)
    def _():
        pl.semaphore_wait(barrier, 3)
        to_north.start()
        to_corner.start()

    @pl.when(lat == 0)
    def _():
        pl.semaphore_wait(barrier, 1)

    to_west.start()
    to_west.wait()

    @pl.when(lat > 0)
    def _():
        to_north.wait_send()
        to_corner.wait_send()

    @pl.when(lat < lat_size - 1)
    def _():
        to_north.wait_recv()
        to_corner.wait_recv()


def gather_kernel(
    slots, mask_ref, where_ref, fields, north, east, corner, own, leaving, info, sems
):
    lat_windows = mask_ref.shape[0]
    lon_windows = fields.shape[1] // WIN_LON
    lat_half, lon_half = WIN_LAT // 2, WIN_LON // 2
    index = where_ref[0]
    first_col = index * lon_windows

    def count(col, total):
        for row in range(lat_windows):
            total = total + mask_ref[row, col]
        return total

    before = lax.fori_loop(0, first_col, count, jnp.int32(0))
    owned = lax.fori_loop(first_col, first_col + lon_windows, count, jnp.int32(0))
    kept = slots - (before - index * slots)
    to_east = before + owned - (index + 1) * slots
    info[0] = kept
    info[1] = slots - to_east - kept

    def fetch(row, col, window, block):
        low_lat, low_lon = row * WIN_LAT + lat_half, col * WIN_LON + lon_half
        last_row, last_col = row == lat_windows - 1, col == lon_windows - 1

        def quarter(source, down, right):
            target = block.at[pl.ds(down, lat_half), pl.ds(right, lon_half)]
            pltpu.make_async_copy(source, target, sems.at[window]).start()

        here = (pl.ds(low_lat, lat_half), pl.ds(low_lon, lon_half))
        quarter(fields.at[here[0], here[1]], 0, 0)

        @pl.when(jnp.logical_not(last_col))
        def _():
            quarter(fields.at[here[0], pl.ds(low_lon + lon_half, lon_half)], 0, lon_half)

        @pl.when(last_col)
        def _():
            quarter(east.at[here[0]], 0, lon_half)

        @pl.when(jnp.logical_not(last_row))
        def _():
            below = pl.ds(low_lat + lat_half, lat_half)
            quarter(fields.at[below, here[1]], lat_half, 0)

            @pl.when(jnp.logical_not(last_col))
            def _():
                quarter(fields.at[below, pl.ds(low_lon + lon_half, lon_half)], lat_half, lon_half)

            @pl.when(last_col)
            def _():
                quarter(east.at[below], lat_half, lon_half)

        @pl.when(last_row)
        def _():
            quarter(north.at[:, here[1]], lat_half, 0)

            @pl.when(jnp.logical_not(last_col))
            def _():
                quarter(north.at[:, pl.ds(low_lon + lon_half, lon_half)], lat_half, lon_half)

            @pl.when(last_col)
            def _():
                quarter(corner, lat_half, lon_half)

    def start(window, rank):
        row, col = window // lon_windows, window % lon_windows
        ocean = mask_ref[row, first_col + col]
        slot = slots - to_east + rank - kept

        @pl.when((ocean == 1) & (rank < kept))
        def _():
            fetch(row, col, window, own.at[rank])

        @pl.when((ocean == 1) & (rank >= kept))
        def _():
            fetch(row, col, window, leaving.at[slot])

        return rank + ocean

    lax.fori_loop(0, lat_windows * lon_windows, start, jnp.int32(0))

    def finish(window, carry):
        row, col = window // lon_windows, window % lon_windows

        @pl.when(mask_ref[row, first_col + col] == 1)
        def _():
            block = fields.at[pl.ds(0, WIN_LAT), pl.ds(0, WIN_LON)]
            pltpu.make_async_copy(block, own.at[0], sems.at[window]).wait()

        return carry

    lax.fori_loop(0, lat_windows * lon_windows, finish, jnp.int32(0))


def place_kernel(
    mask_ref, where_ref, info, finished, returned, result, zero, sems
):
    lat_windows = mask_ref.shape[0]
    lon_windows = result.shape[1] // WIN_LON
    first_col = where_ref[0] * lon_windows
    zero[...] = jnp.zeros_like(zero)
    kept, ahead = info[0], info[1]

    def spot(window):
        row, col = window // lon_windows, window % lon_windows
        return result.at[pl.ds(row * WIN_LAT, WIN_LAT), pl.ds(col * WIN_LON, WIN_LON)]

    def start(window, rank):
        ocean = mask_ref[window // lon_windows, first_col + window % lon_windows]

        @pl.when((ocean == 1) & (rank < kept))
        def _():
            pltpu.make_async_copy(finished.at[rank], spot(window), sems.at[window]).start()

        @pl.when((ocean == 1) & (rank >= kept))
        def _():
            source = returned.at[rank + ahead]
            pltpu.make_async_copy(source, spot(window), sems.at[window]).start()

        @pl.when(ocean == 0)
        def _():
            pltpu.make_async_copy(zero, spot(window), sems.at[window]).start()

        return rank + ocean

    lax.fori_loop(0, lat_windows * lon_windows, start, jnp.int32(0))

    def finish(window, carry):
        pltpu.make_async_copy(zero, spot(window), sems.at[window]).wait()
        return carry

    lax.fori_loop(0, lat_windows * lon_windows, finish, jnp.int32(0))


def normalise(values, gain):
    average = jnp.mean(values, axis=-1, keepdims=True)
    centred = values - average
    spread = jnp.mean(centred * centred, axis=-1, keepdims=True)
    return (centred * lax.rsqrt(spread + NORM_FLOOR) * gain).astype(jnp.bfloat16)


def erf_of(x):
    square = jnp.minimum(x * x, ERF_LIMIT)
    poly = jnp.full_like(square, ERF_COEFS[-1])
    for coef in ERF_COEFS[-2::-1]:
        poly = poly * square + coef
    return jnp.tanh(x * poly)


def dot(left, right):
    return jnp.dot(left, right, preferred_element_type=jnp.float32)


def window_kernel(
    chunk, info, own, leaving, strips, gain_one, w_qkv, w_proj, gain_two, w_up, w_down,
    finished, returned, arrived, bias, block, qkv, mixed,
    out_send, out_recv, back_send, back_recv,
):
    slots = own.shape[0]
    steps = slots // chunk
    heads, group, _ = strips.shape
    features = own.shape[-1]
    tokens = WIN_LAT * group
    dim = features // heads
    kept = info[0]
    scale = LOG2E / math.sqrt(dim)
    lat, lon = lax.axis_index("lat"), lax.axis_index("lon")
    last = lax.axis_size("lon") - 1
    east, west = jnp.minimum(lon + 1, last), jnp.maximum(lon - 1, 0)
    barrier = pltpu.get_barrier_semaphore()

    @pl.when(lon < last)
    def _():
        pl.semaphore_signal(barrier, inc=1, device_id=(lat, east), device_id_type=MESH)

    @pl.when(lon > 0)
    def _():
        pl.semaphore_signal(barrier, inc=1, device_id=(lat, west), device_id_type=MESH)

    @pl.when((lon > 0) & (lon < last))
    def _():
        pl.semaphore_wait(barrier, 2)

    @pl.when((lon == 0) | (lon == last))
    def _():
        pl.semaphore_wait(barrier, 1)

    def part(step):
        return pl.ds((steps - 1 - step) * chunk, chunk)

    def outward(step):
        return pltpu.make_async_remote_copy(
            src_ref=leaving.at[part(step)],
            dst_ref=arrived.at[part(step)],
            send_sem=out_send.at[step],
            recv_sem=out_recv.at[step],
            device_id=(lat, east),
            device_id_type=MESH,
        )

    def homeward(step):
        return pltpu.make_async_remote_copy(
            src_ref=finished.at[part(step)],
            dst_ref=returned.at[part(step)],
            send_sem=back_send.at[step],
            recv_sem=back_recv.at[step],
            device_id=(lat, west),
            device_id_type=MESH,
        )

    @pl.when(lon < last)
    def _():
        for step in range(steps):
            outward(step).start()

    @pl.when(lon == 0)
    def _():
        arrived[...] = jnp.zeros_like(arrived)

    for row in range(WIN_LAT):
        first = (WIN_LAT - 1 - row) * group
        bias[:, row * group : (row + 1) * group, :] = strips[:, :, first : first + tokens]

    lane_head = lax.broadcasted_iota(jnp.int32, (tokens, features), 1) // dim

    def attend(n):
        rows = slice(n * tokens, (n + 1) * tokens)
        query_t = qkv[rows, :features].T
        key = qkv[rows, features : 2 * features]
        value_t = qkv[rows, 2 * features :].T
        masked = [jnp.where(lane_head == h, key, jnp.zeros_like(key)) for h in range(heads)]
        every = dot(jnp.concatenate(masked, axis=0), query_t)
        parts = []
        for h in range(heads):
            scores = every[h * tokens : (h + 1) * tokens] * scale + bias[h]
            power = jnp.exp2(scores - jnp.max(scores, axis=0, keepdims=True))
            total = jnp.sum(power, axis=0, keepdims=True)
            piece = dot(value_t[h * dim : (h + 1) * dim, :], power.astype(jnp.bfloat16))
            parts.append((piece * (1.0 / total)).astype(jnp.bfloat16))
        mixed[rows, :] = jnp.concatenate(parts, axis=0).T

    def compute(step, carry):
        @pl.when(lon > 0)
        def _():
            outward(step).wait_recv()

        base = (steps - 1 - step) * chunk
        for n in range(chunk):
            slot = base + n
            mine = own[slot].reshape(tokens, features)
            other = arrived[slot].reshape(tokens, features)
            block[n * tokens : (n + 1) * tokens, :] = jnp.where(slot < kept, mine, other)
        values = block[...].astype(jnp.float32)
        normed = normalise(values, gain_one[...])
        qkv[...] = dot(normed, w_qkv[...]).astype(jnp.bfloat16)
        for n in range(chunk):
            attend(n)
        middle = (values + dot(mixed[...], w_proj[...])).astype(jnp.bfloat16)
        middle_wide = middle.astype(jnp.float32)
        normed_two = normalise(middle_wide, gain_two[...])
        up = dot(normed_two, w_up[...])
        grown = (0.5 * up * (1.0 + erf_of(up * math.sqrt(0.5)))).astype(jnp.bfloat16)
        result = (middle_wide + dot(grown, w_down[...])).astype(jnp.bfloat16)
        finished[part(step)] = result.reshape((chunk,) + finished.shape[1:])

        @pl.when(lon > 0)
        def _():
            homeward(step).start()

        return carry

    lax.fori_loop(0, steps, compute, 0)

    @pl.when(lon < last)
    def _():
        for step in range(steps):
            outward(step).wait_send()
            homeward(step).wait_recv()

    @pl.when(lon > 0)
    def _():
        for step in range(steps):
            homeward(step).wait_send()


def vmem():
    return pl.BlockSpec(memory_space=pltpu.VMEM)


def smem():
    return pl.BlockSpec(memory_space=pltpu.SMEM)


def any_space():
    return pl.BlockSpec(memory_space=pl.ANY)


def cost(flops, moved):
    return pl.CostEstimate(flops=flops, bytes_accessed=moved, transcendentals=0)


def run_windows(info, own, leaving, strips, gain_one, w_qkv, w_proj, gain_two, w_up, w_down):
    slots, _, _, levels, features = own.shape
    chunk = 2 if slots % 2 == 0 else 1
    heads = strips.shape[0]
    tokens = WIN_LAT * WIN_LON * levels
    flops = 2 * slots * tokens * features * (
        w_qkv.shape[1] + w_proj.shape[1] + 2 * w_up.shape[1] + 4 * tokens
    )
    return pl.pallas_call(
        functools.partial(window_kernel, chunk),
        out_shape=[jax.ShapeDtypeStruct(own.shape, own.dtype)] * 2,
        in_specs=[smem()] + [vmem()] * 9,
        out_specs=[vmem()] * 2,
        scratch_shapes=[
            pltpu.VMEM(own.shape, own.dtype),
            pltpu.VMEM((heads, tokens, tokens), jnp.float32),
            pltpu.VMEM((chunk * tokens, features), jnp.bfloat16),
            pltpu.VMEM((chunk * tokens, 3 * features), jnp.bfloat16),
            pltpu.VMEM((chunk * tokens, features), jnp.bfloat16),
        ]
        + [pltpu.SemaphoreType.DMA((slots // chunk,))] * 4,
        cost_estimate=cost(flops, 4 * own.size),
        compiler_params=pltpu.CompilerParams(
            collective_id=1, has_side_effects=True, vmem_limit_bytes=40 * 2**20
        ),
    )(info, own, leaving, strips, gain_one, w_qkv, w_proj, gain_two, w_up, w_down)


def exchange_halos(fields):
    lat_cells, lon_cells, levels, features = fields.shape
    lat_half, lon_half = WIN_LAT // 2, WIN_LON // 2
    return pl.pallas_call(
        halo_kernel,
        out_shape=[
            jax.ShapeDtypeStruct((lat_half, lon_cells, levels, features), fields.dtype),
            jax.ShapeDtypeStruct((lat_cells, lon_half, levels, features), fields.dtype),
            jax.ShapeDtypeStruct((lat_half, lon_half, levels, features), fields.dtype),
        ],
        in_specs=[any_space()],
        out_specs=[any_space()] * 3,
        scratch_shapes=[pltpu.SemaphoreType.DMA((3,))] * 2,
        cost_estimate=cost(0, fields.size),
        compiler_params=pltpu.CompilerParams(
            collective_id=0, has_side_effects=True, vmem_limit_bytes=2**20
        ),
    )(fields)


def body(fields, ocean_mask, gain_one, w_qkv, rel_bias, w_proj, gain_two, w_up, w_down):
    lat_cells, lon_cells, levels, features = fields.shape
    lat_windows = lat_cells // WIN_LAT
    lon_windows = lon_cells // WIN_LON
    slots = (lat_windows - 1) * lon_windows // 2
    north, east, corner = exchange_halos(fields)
    strips = bias_strips(rel_bias, levels)
    where = jnp.reshape(lax.axis_index("lon"), (1,)).astype(jnp.int32)
    shape = (WIN_LAT, WIN_LON, levels, features)
    window_count = lat_windows * lon_windows
    own, leaving, info = pl.pallas_call(
        functools.partial(gather_kernel, slots),
        out_shape=[
            jax.ShapeDtypeStruct((slots,) + shape, fields.dtype),
            jax.ShapeDtypeStruct((slots,) + shape, fields.dtype),
            jax.ShapeDtypeStruct((2,), jnp.int32),
        ],
        in_specs=[smem(), smem()] + [any_space()] * 4,
        out_specs=[vmem(), vmem(), smem()],
        scratch_shapes=[pltpu.SemaphoreType.DMA((window_count,))],
        cost_estimate=cost(0, 4 * fields.size),
        compiler_params=pltpu.CompilerParams(vmem_limit_bytes=3 * 2**20),
    )(ocean_mask, where, fields, north, east, corner)
    finished, returned = run_windows(
        info, own, leaving, strips, gain_one.reshape(1, -1), w_qkv, w_proj,
        gain_two.reshape(1, -1), w_up, w_down,
    )
    return pl.pallas_call(
        place_kernel,
        out_shape=jax.ShapeDtypeStruct(fields.shape, fields.dtype),
        in_specs=[smem()] * 3 + [any_space()] * 2,
        out_specs=any_space(),
        scratch_shapes=[
            pltpu.VMEM(shape, fields.dtype),
            pltpu.SemaphoreType.DMA((window_count,)),
        ],
        cost_estimate=cost(0, 4 * fields.size),
        compiler_params=pltpu.CompilerParams(vmem_limit_bytes=2**20),
    )(ocean_mask, where, info, finished, returned)


def solution(mesh):
    in_specs = (P("lat", "lon", None, None), P("lat", None), P(), P(), P(), P(), P(), P(), P())
    out_specs = P("lat", "lon", None, None)
    return jax.shard_map(body, mesh=mesh, in_specs=in_specs, out_specs=out_specs, check_vma=False)
```

```python
import functools
import math

import jax
import jax.numpy as jnp
from jax import lax
from jax.experimental import pallas as pl
from jax.experimental.pallas import tpu as pltpu
from jax.sharding import PartitionSpec as P

WIN_LAT = 8
WIN_LON = 8
NORM_FLOOR = 0.25
MESH = pl.DeviceIdType.MESH
LOG2E = math.log2(math.e)
ERF_COEFS = (1.1283793294596702, 0.10276689183983656, -0.0001854270054620651, -0.000625856981717449, 9.00024455627471e-05, -6.058558938836915e-06, 1.6416008301278458e-07)
ERF_LIMIT = 15.209999999999999


def bias_strips(rel_bias, padded, strips, levels):
    heads, length = rel_bias.shape
    col_step = 2 * levels - 1
    row_step = (2 * WIN_LON - 1) * col_step
    offsets = [c * col_step + lev for c in range(WIN_LON) for lev in range(levels)]
    top = offsets[-1]
    width = padded.shape[1] - 128
    padded[...] = jnp.zeros_like(padded)
    padded[:, :length] = rel_bias[...] * LOG2E
    table = padded[...]
    left = jnp.concatenate([table[:, top - q : top - q + width] for q in offsets], axis=0)
    group = WIN_LON * levels
    lane = lax.broadcasted_iota(jnp.int32, (width, strips.shape[2]), 1)
    inner = lane % group
    target = lane // group * row_step + inner // levels * col_step + inner % levels
    pick = lax.broadcasted_iota(jnp.int32, target.shape, 0) == target
    found = jnp.dot(
        left,
        pick.astype(jnp.float32),
        precision=lax.Precision.HIGHEST,
        preferred_element_type=jnp.float32,
    )
    for place in range(group):
        strips[:, place, :] = found[place * heads : (place + 1) * heads]


def halo_kernel(fields, rel_bias, north, east, corner, strips, padded, send_sems, recv_sems):
    lat_half, lon_half = WIN_LAT // 2, WIN_LON // 2
    lat, lon = lax.axis_index("lat"), lax.axis_index("lon")
    lat_size, lon_size = lax.axis_size("lat"), lax.axis_size("lon")
    west, east_of = (lon + lon_size - 1) % lon_size, (lon + 1) % lon_size
    barrier = pltpu.get_barrier_semaphore()

    def greet(row, col):
        pl.semaphore_signal(barrier, inc=1, device_id=(row, col), device_id_type=MESH)

    greet(lat, east_of)

    @pl.when(lat < lat_size - 1)
    def _():
        greet(lat + 1, lon)
        greet(lat + 1, east_of)

    def transfer(which, source, target, row, col):
        return pltpu.make_async_remote_copy(
            src_ref=source,
            dst_ref=target,
            send_sem=send_sems.at[which],
            recv_sem=recv_sems.at[which],
            device_id=(row, col),
            device_id_type=MESH,
        )

    up = jnp.maximum(lat - 1, 0)
    to_west = transfer(0, fields.at[:, pl.ds(0, lon_half)], east, lat, west)
    to_north = transfer(1, fields.at[pl.ds(0, lat_half)], north, up, lon)
    to_corner = transfer(
        2, fields.at[pl.ds(0, lat_half), pl.ds(0, lon_half)], corner, up, west
    )

    @pl.when(lat > 0)
    def _():
        pl.semaphore_wait(barrier, 3)
        to_north.start()
        to_corner.start()

    @pl.when(lat == 0)
    def _():
        pl.semaphore_wait(barrier, 1)

    to_west.start()
    bias_strips(rel_bias, padded, strips, fields.shape[2])
    to_west.wait()

    @pl.when(lat > 0)
    def _():
        to_north.wait_send()
        to_corner.wait_send()

    @pl.when(lat < lat_size - 1)
    def _():
        to_north.wait_recv()
        to_corner.wait_recv()


def gather_kernel(
    slots, mask_ref, where_ref, fields, north, east, corner, own, leaving, info, sems
):
    lat_windows = mask_ref.shape[0]
    lon_windows = fields.shape[1] // WIN_LON
    lat_half, lon_half = WIN_LAT // 2, WIN_LON // 2
    index = where_ref[0]
    first_col = index * lon_windows

    def count(col, total):
        for row in range(lat_windows):
            total = total + mask_ref[row, col]
        return total

    before = lax.fori_loop(0, first_col, count, jnp.int32(0))
    owned = lax.fori_loop(first_col, first_col + lon_windows, count, jnp.int32(0))
    kept = slots - (before - index * slots)
    to_east = before + owned - (index + 1) * slots
    info[0] = kept
    info[1] = slots - to_east - kept

    def fetch(row, col, window, block):
        low_lat, low_lon = row * WIN_LAT + lat_half, col * WIN_LON + lon_half
        last_row, last_col = row == lat_windows - 1, col == lon_windows - 1

        def quarter(source, down, right):
            target = block.at[pl.ds(down, lat_half), pl.ds(right, lon_half)]
            pltpu.make_async_copy(source, target, sems.at[window]).start()

        here = (pl.ds(low_lat, lat_half), pl.ds(low_lon, lon_half))
        quarter(fields.at[here[0], here[1]], 0, 0)

        @pl.when(jnp.logical_not(last_col))
        def _():
            quarter(fields.at[here[0], pl.ds(low_lon + lon_half, lon_half)], 0, lon_half)

        @pl.when(last_col)
        def _():
            quarter(east.at[here[0]], 0, lon_half)

        @pl.when(jnp.logical_not(last_row))
        def _():
            below = pl.ds(low_lat + lat_half, lat_half)
            quarter(fields.at[below, here[1]], lat_half, 0)

            @pl.when(jnp.logical_not(last_col))
            def _():
                quarter(fields.at[below, pl.ds(low_lon + lon_half, lon_half)], lat_half, lon_half)

            @pl.when(last_col)
            def _():
                quarter(east.at[below], lat_half, lon_half)

        @pl.when(last_row)
        def _():
            quarter(north.at[:, here[1]], lat_half, 0)

            @pl.when(jnp.logical_not(last_col))
            def _():
                quarter(north.at[:, pl.ds(low_lon + lon_half, lon_half)], lat_half, lon_half)

            @pl.when(last_col)
            def _():
                quarter(corner, lat_half, lon_half)

    def start(window, rank):
        row, col = window // lon_windows, window % lon_windows
        ocean = mask_ref[row, first_col + col]
        slot = slots - to_east + rank - kept

        @pl.when((ocean == 1) & (rank < kept))
        def _():
            fetch(row, col, window, own.at[rank])

        @pl.when((ocean == 1) & (rank >= kept))
        def _():
            fetch(row, col, window, leaving.at[slot])

        return rank + ocean

    lax.fori_loop(0, lat_windows * lon_windows, start, jnp.int32(0))

    def finish(window, carry):
        row, col = window // lon_windows, window % lon_windows

        @pl.when(mask_ref[row, first_col + col] == 1)
        def _():
            block = fields.at[pl.ds(0, WIN_LAT), pl.ds(0, WIN_LON)]
            pltpu.make_async_copy(block, own.at[0], sems.at[window]).wait()

        return carry

    lax.fori_loop(0, lat_windows * lon_windows, finish, jnp.int32(0))


def place_kernel(
    mask_ref, where_ref, info, finished, returned, result, zero, sems
):
    lat_windows = mask_ref.shape[0]
    lon_windows = result.shape[1] // WIN_LON
    first_col = where_ref[0] * lon_windows
    zero[...] = jnp.zeros_like(zero)
    kept, ahead = info[0], info[1]

    def spot(window):
        row, col = window // lon_windows, window % lon_windows
        return result.at[pl.ds(row * WIN_LAT, WIN_LAT), pl.ds(col * WIN_LON, WIN_LON)]

    def start(window, rank):
        ocean = mask_ref[window // lon_windows, first_col + window % lon_windows]

        @pl.when((ocean == 1) & (rank < kept))
        def _():
            pltpu.make_async_copy(finished.at[rank], spot(window), sems.at[window]).start()

        @pl.when((ocean == 1) & (rank >= kept))
        def _():
            source = returned.at[rank + ahead]
            pltpu.make_async_copy(source, spot(window), sems.at[window]).start()

        @pl.when(ocean == 0)
        def _():
            pltpu.make_async_copy(zero, spot(window), sems.at[window]).start()

        return rank + ocean

    lax.fori_loop(0, lat_windows * lon_windows, start, jnp.int32(0))

    def finish(window, carry):
        pltpu.make_async_copy(zero, spot(window), sems.at[window]).wait()
        return carry

    lax.fori_loop(0, lat_windows * lon_windows, finish, jnp.int32(0))


def normalise(values, gain):
    average = jnp.mean(values, axis=-1, keepdims=True)
    centred = values - average
    spread = jnp.mean(centred * centred, axis=-1, keepdims=True)
    return (centred * lax.rsqrt(spread + NORM_FLOOR) * gain).astype(jnp.bfloat16)


def erf_of(x):
    square = jnp.minimum(x * x, ERF_LIMIT)
    poly = jnp.full_like(square, ERF_COEFS[-1])
    for coef in ERF_COEFS[-2::-1]:
        poly = poly * square + coef
    return jnp.tanh(x * poly)


def dot(left, right):
    return jnp.dot(left, right, preferred_element_type=jnp.float32)


def window_kernel(
    chunk, info, own, leaving, strips, gain_one, w_qkv, w_proj, gain_two, w_up, w_down,
    finished, returned, arrived, bias, block, qkv, mixed,
    out_send, out_recv, back_send, back_recv,
):
    slots = own.shape[0]
    steps = slots // chunk
    heads, group, _ = strips.shape
    features = own.shape[-1]
    tokens = WIN_LAT * group
    dim = features // heads
    kept = info[0]
    scale = LOG2E / math.sqrt(dim)
    lat, lon = lax.axis_index("lat"), lax.axis_index("lon")
    last = lax.axis_size("lon") - 1
    east, west = jnp.minimum(lon + 1, last), jnp.maximum(lon - 1, 0)
    barrier = pltpu.get_barrier_semaphore()

    @pl.when(lon < last)
    def _():
        pl.semaphore_signal(barrier, inc=1, device_id=(lat, east), device_id_type=MESH)

    @pl.when(lon > 0)
    def _():
        pl.semaphore_signal(barrier, inc=1, device_id=(lat, west), device_id_type=MESH)

    @pl.when((lon > 0) & (lon < last))
    def _():
        pl.semaphore_wait(barrier, 2)

    @pl.when((lon == 0) | (lon == last))
    def _():
        pl.semaphore_wait(barrier, 1)

    def part(step):
        return pl.ds((steps - 1 - step) * chunk, chunk)

    def outward(step):
        return pltpu.make_async_remote_copy(
            src_ref=leaving.at[part(step)],
            dst_ref=arrived.at[part(step)],
            send_sem=out_send.at[step],
            recv_sem=out_recv.at[step],
            device_id=(lat, east),
            device_id_type=MESH,
        )

    def homeward(step):
        return pltpu.make_async_remote_copy(
            src_ref=finished.at[part(step)],
            dst_ref=returned.at[part(step)],
            send_sem=back_send.at[step],
            recv_sem=back_recv.at[step],
            device_id=(lat, west),
            device_id_type=MESH,
        )

    @pl.when(lon < last)
    def _():
        for step in range(steps):
            outward(step).start()

    @pl.when(lon == 0)
    def _():
        arrived[...] = jnp.zeros_like(arrived)

    for row in range(WIN_LAT):
        first = (WIN_LAT - 1 - row) * group
        bias[:, row * group : (row + 1) * group, :] = strips[:, :, first : first + tokens]

    lane_head = lax.broadcasted_iota(jnp.int32, (tokens, features), 1) // dim

    def attend(n):
        rows = slice(n * tokens, (n + 1) * tokens)
        query_t = qkv[rows, :features].T
        key = qkv[rows, features : 2 * features]
        value_t = qkv[rows, 2 * features :].T
        masked = [jnp.where(lane_head == h, key, jnp.zeros_like(key)) for h in range(heads)]
        every = dot(jnp.concatenate(masked, axis=0), query_t)
        parts = []
        for h in range(heads):
            scores = every[h * tokens : (h + 1) * tokens] * scale + bias[h]
            power = jnp.exp2(scores - jnp.max(scores, axis=0, keepdims=True))
            total = jnp.sum(power, axis=0, keepdims=True)
            piece = dot(value_t[h * dim : (h + 1) * dim, :], power.astype(jnp.bfloat16))
            parts.append((piece * (1.0 / total)).astype(jnp.bfloat16))
        mixed[rows, :] = jnp.concatenate(parts, axis=0).T

    def compute(step, carry):
        @pl.when(lon > 0)
        def _():
            outward(step).wait_recv()

        base = (steps - 1 - step) * chunk
        for n in range(chunk):
            slot = base + n
            mine = own[slot].reshape(tokens, features)
            other = arrived[slot].reshape(tokens, features)
            block[n * tokens : (n + 1) * tokens, :] = jnp.where(slot < kept, mine, other)
        values = block[...].astype(jnp.float32)
        normed = normalise(values, gain_one[...])
        qkv[...] = dot(normed, w_qkv[...]).astype(jnp.bfloat16)
        for n in range(chunk):
            attend(n)
        middle = (values + dot(mixed[...], w_proj[...])).astype(jnp.bfloat16)
        middle_wide = middle.astype(jnp.float32)
        normed_two = normalise(middle_wide, gain_two[...])
        up = dot(normed_two, w_up[...])
        grown = (0.5 * up * (1.0 + erf_of(up * math.sqrt(0.5)))).astype(jnp.bfloat16)
        result = (middle_wide + dot(grown, w_down[...])).astype(jnp.bfloat16)
        finished[part(step)] = result.reshape((chunk,) + finished.shape[1:])

        @pl.when(lon > 0)
        def _():
            homeward(step).start()

        return carry

    lax.fori_loop(0, steps, compute, 0)

    @pl.when(lon < last)
    def _():
        for step in range(steps):
            outward(step).wait_send()
            homeward(step).wait_recv()

    @pl.when(lon > 0)
    def _():
        for step in range(steps):
            homeward(step).wait_send()


def vmem():
    return pl.BlockSpec(memory_space=pltpu.VMEM)


def smem():
    return pl.BlockSpec(memory_space=pltpu.SMEM)


def any_space():
    return pl.BlockSpec(memory_space=pl.ANY)


def cost(flops, moved):
    return pl.CostEstimate(flops=flops, bytes_accessed=moved, transcendentals=0)


def run_windows(info, own, leaving, strips, gain_one, w_qkv, w_proj, gain_two, w_up, w_down):
    slots, _, _, levels, features = own.shape
    chunk = 2 if slots % 2 == 0 else 1
    heads = strips.shape[0]
    tokens = WIN_LAT * WIN_LON * levels
    flops = 2 * slots * tokens * features * (
        w_qkv.shape[1] + w_proj.shape[1] + 2 * w_up.shape[1] + 4 * tokens
    )
    return pl.pallas_call(
        functools.partial(window_kernel, chunk),
        out_shape=[jax.ShapeDtypeStruct(own.shape, own.dtype)] * 2,
        in_specs=[smem()] + [vmem()] * 9,
        out_specs=[vmem()] * 2,
        scratch_shapes=[
            pltpu.VMEM(own.shape, own.dtype),
            pltpu.VMEM((heads, tokens, tokens), jnp.float32),
            pltpu.VMEM((chunk * tokens, features), jnp.bfloat16),
            pltpu.VMEM((chunk * tokens, 3 * features), jnp.bfloat16),
            pltpu.VMEM((chunk * tokens, features), jnp.bfloat16),
        ]
        + [pltpu.SemaphoreType.DMA((slots // chunk,))] * 4,
        cost_estimate=cost(flops, 4 * own.size),
        compiler_params=pltpu.CompilerParams(
            collective_id=1, has_side_effects=True, vmem_limit_bytes=40 * 2**20
        ),
    )(info, own, leaving, strips, gain_one, w_qkv, w_proj, gain_two, w_up, w_down)


def exchange_halos(fields, rel_bias):
    lat_cells, lon_cells, levels, features = fields.shape
    lat_half, lon_half = WIN_LAT // 2, WIN_LON // 2
    heads, length = rel_bias.shape
    group = WIN_LON * levels
    return pl.pallas_call(
        halo_kernel,
        out_shape=[
            jax.ShapeDtypeStruct((lat_half, lon_cells, levels, features), fields.dtype),
            jax.ShapeDtypeStruct((lat_cells, lon_half, levels, features), fields.dtype),
            jax.ShapeDtypeStruct((lat_half, lon_half, levels, features), fields.dtype),
            jax.ShapeDtypeStruct((heads, group, 2 * WIN_LAT * group), jnp.float32),
        ],
        in_specs=[pl.BlockSpec(memory_space=pltpu.HBM), vmem()],
        out_specs=[any_space()] * 3 + [vmem()],
        scratch_shapes=[pltpu.VMEM((heads, (length + 255) // 128 * 128), jnp.float32)]
        + [pltpu.SemaphoreType.DMA((3,))] * 2,
        cost_estimate=cost(0, fields.size),
        compiler_params=pltpu.CompilerParams(
            collective_id=0, has_side_effects=True, vmem_limit_bytes=4 * 2**20
        ),
    )(fields, rel_bias)


def body(fields, ocean_mask, gain_one, w_qkv, rel_bias, w_proj, gain_two, w_up, w_down):
    lat_cells, lon_cells, levels, features = fields.shape
    lat_windows = lat_cells // WIN_LAT
    lon_windows = lon_cells // WIN_LON
    slots = (lat_windows - 1) * lon_windows // 2
    north, east, corner, strips = exchange_halos(fields, rel_bias)
    where = jnp.reshape(lax.axis_index("lon"), (1,)).astype(jnp.int32)
    shape = (WIN_LAT, WIN_LON, levels, features)
    window_count = lat_windows * lon_windows
    own, leaving, info = pl.pallas_call(
        functools.partial(gather_kernel, slots),
        out_shape=[
            jax.ShapeDtypeStruct((slots,) + shape, fields.dtype),
            jax.ShapeDtypeStruct((slots,) + shape, fields.dtype),
            jax.ShapeDtypeStruct((2,), jnp.int32),
        ],
        in_specs=[smem(), smem()] + [any_space()] * 4,
        out_specs=[vmem(), vmem(), smem()],
        scratch_shapes=[pltpu.SemaphoreType.DMA((window_count,))],
        cost_estimate=cost(0, 4 * fields.size),
        compiler_params=pltpu.CompilerParams(vmem_limit_bytes=3 * 2**20),
    )(ocean_mask, where, fields, north, east, corner)
    finished, returned = run_windows(
        info, own, leaving, strips, gain_one.reshape(1, -1), w_qkv, w_proj,
        gain_two.reshape(1, -1), w_up, w_down,
    )
    return pl.pallas_call(
        place_kernel,
        out_shape=jax.ShapeDtypeStruct(fields.shape, fields.dtype),
        in_specs=[smem()] * 3 + [any_space()] * 2,
        out_specs=any_space(),
        scratch_shapes=[
            pltpu.VMEM(shape, fields.dtype),
            pltpu.SemaphoreType.DMA((window_count,)),
        ],
        cost_estimate=cost(0, 4 * fields.size),
        compiler_params=pltpu.CompilerParams(vmem_limit_bytes=2**20),
    )(ocean_mask, where, info, finished, returned)


def solution(mesh):
    in_specs = (P("lat", "lon", None, None), P("lat", None), P(), P(), P(), P(), P(), P(), P())
    out_specs = P("lat", "lon", None, None)
    return jax.shard_map(body, mesh=mesh, in_specs=in_specs, out_specs=out_specs, check_vma=False)
```

```python
import functools
import math

import jax
import jax.numpy as jnp
from jax import lax
from jax.experimental import pallas as pl
from jax.experimental.pallas import tpu as pltpu
from jax.sharding import PartitionSpec as P

WIN_LAT = 8
WIN_LON = 8
NORM_FLOOR = 0.25
MESH = pl.DeviceIdType.MESH
LOG2E = math.log2(math.e)
ERF_COEFS = (1.1283793294596702, 0.10276689183983656, -0.0001854270054620651, -0.000625856981717449, 9.00024455627471e-05, -6.058558938836915e-06, 1.6416008301278458e-07)
ERF_LIMIT = 15.209999999999999


def bias_strips(rel_bias, padded, strips, levels):
    heads, length = rel_bias.shape
    col_step = 2 * levels - 1
    row_step = (2 * WIN_LON - 1) * col_step
    offsets = [c * col_step + lev for c in range(WIN_LON) for lev in range(levels)]
    top = offsets[-1]
    width = padded.shape[1] - 128
    padded[...] = jnp.zeros_like(padded)
    padded[:, :length] = rel_bias[...] * LOG2E
    table = padded[...]
    left = jnp.concatenate([table[:, top - q : top - q + width] for q in offsets], axis=0)
    group = WIN_LON * levels
    lane = lax.broadcasted_iota(jnp.int32, (width, strips.shape[2]), 1)
    inner = lane % group
    target = lane // group * row_step + inner // levels * col_step + inner % levels
    pick = lax.broadcasted_iota(jnp.int32, target.shape, 0) == target
    found = jnp.dot(
        left,
        pick.astype(jnp.float32),
        precision=lax.Precision.HIGHEST,
        preferred_element_type=jnp.float32,
    )
    for place in range(group):
        strips[:, place, :] = found[place * heads : (place + 1) * heads]


def halo_kernel(fields, north, east, corner, send_sems, recv_sems):
    lat_half, lon_half = WIN_LAT // 2, WIN_LON // 2
    lat, lon = lax.axis_index("lat"), lax.axis_index("lon")
    lat_size, lon_size = lax.axis_size("lat"), lax.axis_size("lon")
    west, east_of = (lon + lon_size - 1) % lon_size, (lon + 1) % lon_size
    barrier = pltpu.get_barrier_semaphore()

    def greet(row, col):
        pl.semaphore_signal(barrier, inc=1, device_id=(row, col), device_id_type=MESH)

    greet(lat, east_of)

    @pl.when(lat < lat_size - 1)
    def _():
        greet(lat + 1, lon)
        greet(lat + 1, east_of)

    def transfer(which, source, target, row, col):
        return pltpu.make_async_remote_copy(
            src_ref=source,
            dst_ref=target,
            send_sem=send_sems.at[which],
            recv_sem=recv_sems.at[which],
            device_id=(row, col),
            device_id_type=MESH,
        )

    up = jnp.maximum(lat - 1, 0)
    to_west = transfer(0, fields.at[:, pl.ds(0, lon_half)], east, lat, west)
    to_north = transfer(1, fields.at[pl.ds(0, lat_half)], north, up, lon)
    to_corner = transfer(
        2, fields.at[pl.ds(0, lat_half), pl.ds(0, lon_half)], corner, up, west
    )

    @pl.when(lat > 0)
    def _():
        pl.semaphore_wait(barrier, 3)
        to_north.start()
        to_corner.start()

    @pl.when(lat == 0)
    def _():
        pl.semaphore_wait(barrier, 1)

    to_west.start()
    to_west.wait()

    @pl.when(lat > 0)
    def _():
        to_north.wait_send()
        to_corner.wait_send()

    @pl.when(lat < lat_size - 1)
    def _():
        to_north.wait_recv()
        to_corner.wait_recv()


def gather_kernel(
    slots, mask_ref, where_ref, rel_bias, fields, north, east, corner,
    own, leaving, info, strips, padded, sems,
):
    lat_windows = mask_ref.shape[0]
    lon_windows = fields.shape[1] // WIN_LON
    lat_half, lon_half = WIN_LAT // 2, WIN_LON // 2
    index = where_ref[0]
    first_col = index * lon_windows

    def count(col, total):
        for row in range(lat_windows):
            total = total + mask_ref[row, col]
        return total

    before = lax.fori_loop(0, first_col, count, jnp.int32(0))
    owned = lax.fori_loop(first_col, first_col + lon_windows, count, jnp.int32(0))
    kept = slots - (before - index * slots)
    to_east = before + owned - (index + 1) * slots
    info[0] = kept
    info[1] = slots - to_east - kept

    def fetch(row, col, window, block):
        low_lat, low_lon = row * WIN_LAT + lat_half, col * WIN_LON + lon_half
        last_row, last_col = row == lat_windows - 1, col == lon_windows - 1

        def quarter(source, down, right):
            target = block.at[pl.ds(down, lat_half), pl.ds(right, lon_half)]
            pltpu.make_async_copy(source, target, sems.at[window]).start()

        here = (pl.ds(low_lat, lat_half), pl.ds(low_lon, lon_half))
        quarter(fields.at[here[0], here[1]], 0, 0)

        @pl.when(jnp.logical_not(last_col))
        def _():
            quarter(fields.at[here[0], pl.ds(low_lon + lon_half, lon_half)], 0, lon_half)

        @pl.when(last_col)
        def _():
            quarter(east.at[here[0]], 0, lon_half)

        @pl.when(jnp.logical_not(last_row))
        def _():
            below = pl.ds(low_lat + lat_half, lat_half)
            quarter(fields.at[below, here[1]], lat_half, 0)

            @pl.when(jnp.logical_not(last_col))
            def _():
                quarter(fields.at[below, pl.ds(low_lon + lon_half, lon_half)], lat_half, lon_half)

            @pl.when(last_col)
            def _():
                quarter(east.at[below], lat_half, lon_half)

        @pl.when(last_row)
        def _():
            quarter(north.at[:, here[1]], lat_half, 0)

            @pl.when(jnp.logical_not(last_col))
            def _():
                quarter(north.at[:, pl.ds(low_lon + lon_half, lon_half)], lat_half, lon_half)

            @pl.when(last_col)
            def _():
                quarter(corner, lat_half, lon_half)

    def start(window, rank):
        row, col = window // lon_windows, window % lon_windows
        ocean = mask_ref[row, first_col + col]
        slot = slots - to_east + rank - kept

        @pl.when((ocean == 1) & (rank < kept))
        def _():
            fetch(row, col, window, own.at[rank])

        @pl.when((ocean == 1) & (rank >= kept))
        def _():
            fetch(row, col, window, leaving.at[slot])

        return rank + ocean

    lax.fori_loop(0, lat_windows * lon_windows, start, jnp.int32(0))

    bias_strips(rel_bias, padded, strips, fields.shape[2])

    def finish(window, carry):
        row, col = window // lon_windows, window % lon_windows

        @pl.when(mask_ref[row, first_col + col] == 1)
        def _():
            block = fields.at[pl.ds(0, WIN_LAT), pl.ds(0, WIN_LON)]
            pltpu.make_async_copy(block, own.at[0], sems.at[window]).wait()

        return carry

    lax.fori_loop(0, lat_windows * lon_windows, finish, jnp.int32(0))


def place_kernel(
    mask_ref, where_ref, info, finished, returned, result, zero, sems
):
    lat_windows = mask_ref.shape[0]
    lon_windows = result.shape[1] // WIN_LON
    first_col = where_ref[0] * lon_windows
    zero[...] = jnp.zeros_like(zero)
    kept, ahead = info[0], info[1]

    def spot(window):
        row, col = window // lon_windows, window % lon_windows
        return result.at[pl.ds(row * WIN_LAT, WIN_LAT), pl.ds(col * WIN_LON, WIN_LON)]

    def start(window, rank):
        ocean = mask_ref[window // lon_windows, first_col + window % lon_windows]

        @pl.when((ocean == 1) & (rank < kept))
        def _():
            pltpu.make_async_copy(finished.at[rank], spot(window), sems.at[window]).start()

        @pl.when((ocean == 1) & (rank >= kept))
        def _():
            source = returned.at[rank + ahead]
            pltpu.make_async_copy(source, spot(window), sems.at[window]).start()

        @pl.when(ocean == 0)
        def _():
            pltpu.make_async_copy(zero, spot(window), sems.at[window]).start()

        return rank + ocean

    lax.fori_loop(0, lat_windows * lon_windows, start, jnp.int32(0))

    def finish(window, carry):
        pltpu.make_async_copy(zero, spot(window), sems.at[window]).wait()
        return carry

    lax.fori_loop(0, lat_windows * lon_windows, finish, jnp.int32(0))


def normalise(values, gain):
    average = jnp.mean(values, axis=-1, keepdims=True)
    centred = values - average
    spread = jnp.mean(centred * centred, axis=-1, keepdims=True)
    return (centred * lax.rsqrt(spread + NORM_FLOOR) * gain).astype(jnp.bfloat16)


def erf_of(x):
    square = jnp.minimum(x * x, ERF_LIMIT)
    poly = jnp.full_like(square, ERF_COEFS[-1])
    for coef in ERF_COEFS[-2::-1]:
        poly = poly * square + coef
    return jnp.tanh(x * poly)


def dot(left, right):
    return jnp.dot(left, right, preferred_element_type=jnp.float32)


def window_kernel(
    chunk, info, own, leaving, strips, gain_one, w_qkv, w_proj, gain_two, w_up, w_down,
    finished, returned, arrived, bias, block, qkv, mixed,
    out_send, out_recv, back_send, back_recv,
):
    slots = own.shape[0]
    steps = slots // chunk
    heads, group, _ = strips.shape
    features = own.shape[-1]
    tokens = WIN_LAT * group
    dim = features // heads
    kept = info[0]
    scale = LOG2E / math.sqrt(dim)
    lat, lon = lax.axis_index("lat"), lax.axis_index("lon")
    last = lax.axis_size("lon") - 1
    east, west = jnp.minimum(lon + 1, last), jnp.maximum(lon - 1, 0)
    barrier = pltpu.get_barrier_semaphore()

    @pl.when(lon < last)
    def _():
        pl.semaphore_signal(barrier, inc=1, device_id=(lat, east), device_id_type=MESH)

    @pl.when(lon > 0)
    def _():
        pl.semaphore_signal(barrier, inc=1, device_id=(lat, west), device_id_type=MESH)

    @pl.when((lon > 0) & (lon < last))
    def _():
        pl.semaphore_wait(barrier, 2)

    @pl.when((lon == 0) | (lon == last))
    def _():
        pl.semaphore_wait(barrier, 1)

    def part(step):
        return pl.ds((steps - 1 - step) * chunk, chunk)

    def outward(step):
        return pltpu.make_async_remote_copy(
            src_ref=leaving.at[part(step)],
            dst_ref=arrived.at[part(step)],
            send_sem=out_send.at[step],
            recv_sem=out_recv.at[step],
            device_id=(lat, east),
            device_id_type=MESH,
        )

    def homeward(step):
        return pltpu.make_async_remote_copy(
            src_ref=finished.at[part(step)],
            dst_ref=returned.at[part(step)],
            send_sem=back_send.at[step],
            recv_sem=back_recv.at[step],
            device_id=(lat, west),
            device_id_type=MESH,
        )

    @pl.when(lon < last)
    def _():
        for step in range(steps):
            outward(step).start()

    @pl.when(lon == 0)
    def _():
        arrived[...] = jnp.zeros_like(arrived)

    for row in range(WIN_LAT):
        first = (WIN_LAT - 1 - row) * group
        bias[:, row * group : (row + 1) * group, :] = strips[:, :, first : first + tokens]

    lane_head = lax.broadcasted_iota(jnp.int32, (tokens, features), 1) // dim

    def attend(n):
        rows = slice(n * tokens, (n + 1) * tokens)
        query_t = qkv[rows, :features].T
        key = qkv[rows, features : 2 * features]
        value_t = qkv[rows, 2 * features :].T
        masked = [jnp.where(lane_head == h, key, jnp.zeros_like(key)) for h in range(heads)]
        every = dot(jnp.concatenate(masked, axis=0), query_t)
        parts = []
        for h in range(heads):
            scores = every[h * tokens : (h + 1) * tokens] * scale + bias[h]
            power = jnp.exp2(scores - jnp.max(scores, axis=0, keepdims=True))
            total = jnp.sum(power, axis=0, keepdims=True)
            piece = dot(value_t[h * dim : (h + 1) * dim, :], power.astype(jnp.bfloat16))
            parts.append((piece * (1.0 / total)).astype(jnp.bfloat16))
        mixed[rows, :] = jnp.concatenate(parts, axis=0).T

    def compute(step, carry):
        @pl.when(lon > 0)
        def _():
            outward(step).wait_recv()

        base = (steps - 1 - step) * chunk
        for n in range(chunk):
            slot = base + n
            mine = own[slot].reshape(tokens, features)
            other = arrived[slot].reshape(tokens, features)
            block[n * tokens : (n + 1) * tokens, :] = jnp.where(slot < kept, mine, other)
        values = block[...].astype(jnp.float32)
        normed = normalise(values, gain_one[...])
        qkv[...] = dot(normed, w_qkv[...]).astype(jnp.bfloat16)
        for n in range(chunk):
            attend(n)
        middle = (values + dot(mixed[...], w_proj[...])).astype(jnp.bfloat16)
        middle_wide = middle.astype(jnp.float32)
        normed_two = normalise(middle_wide, gain_two[...])
        up = dot(normed_two, w_up[...])
        grown = (0.5 * up * (1.0 + erf_of(up * math.sqrt(0.5)))).astype(jnp.bfloat16)
        result = (middle_wide + dot(grown, w_down[...])).astype(jnp.bfloat16)
        finished[part(step)] = result.reshape((chunk,) + finished.shape[1:])

        @pl.when(lon > 0)
        def _():
            homeward(step).start()

        return carry

    lax.fori_loop(0, steps, compute, 0)

    @pl.when(lon < last)
    def _():
        for step in range(steps):
            outward(step).wait_send()
            homeward(step).wait_recv()

    @pl.when(lon > 0)
    def _():
        for step in range(steps):
            homeward(step).wait_send()


def vmem():
    return pl.BlockSpec(memory_space=pltpu.VMEM)


def smem():
    return pl.BlockSpec(memory_space=pltpu.SMEM)


def any_space():
    return pl.BlockSpec(memory_space=pl.ANY)


def cost(flops, moved):
    return pl.CostEstimate(flops=flops, bytes_accessed=moved, transcendentals=0)


def run_windows(info, own, leaving, strips, gain_one, w_qkv, w_proj, gain_two, w_up, w_down):
    slots, _, _, levels, features = own.shape
    chunk = 2 if slots % 2 == 0 else 1
    heads = strips.shape[0]
    tokens = WIN_LAT * WIN_LON * levels
    flops = 2 * slots * tokens * features * (
        w_qkv.shape[1] + w_proj.shape[1] + 2 * w_up.shape[1] + 4 * tokens
    )
    return pl.pallas_call(
        functools.partial(window_kernel, chunk),
        out_shape=[jax.ShapeDtypeStruct(own.shape, own.dtype)] * 2,
        in_specs=[smem()] + [vmem()] * 9,
        out_specs=[vmem()] * 2,
        scratch_shapes=[
            pltpu.VMEM(own.shape, own.dtype),
            pltpu.VMEM((heads, tokens, tokens), jnp.float32),
            pltpu.VMEM((chunk * tokens, features), jnp.bfloat16),
            pltpu.VMEM((chunk * tokens, 3 * features), jnp.bfloat16),
            pltpu.VMEM((chunk * tokens, features), jnp.bfloat16),
        ]
        + [pltpu.SemaphoreType.DMA((slots // chunk,))] * 4,
        cost_estimate=cost(flops, 4 * own.size),
        compiler_params=pltpu.CompilerParams(
            collective_id=1, has_side_effects=True, vmem_limit_bytes=40 * 2**20
        ),
    )(info, own, leaving, strips, gain_one, w_qkv, w_proj, gain_two, w_up, w_down)


def exchange_halos(fields):
    lat_cells, lon_cells, levels, features = fields.shape
    lat_half, lon_half = WIN_LAT // 2, WIN_LON // 2
    return pl.pallas_call(
        halo_kernel,
        out_shape=[
            jax.ShapeDtypeStruct((lat_half, lon_cells, levels, features), fields.dtype),
            jax.ShapeDtypeStruct((lat_cells, lon_half, levels, features), fields.dtype),
            jax.ShapeDtypeStruct((lat_half, lon_half, levels, features), fields.dtype),
        ],
        in_specs=[any_space()],
        out_specs=[any_space()] * 3,
        scratch_shapes=[pltpu.SemaphoreType.DMA((3,))] * 2,
        cost_estimate=cost(0, fields.size),
        compiler_params=pltpu.CompilerParams(
            collective_id=0, has_side_effects=True, vmem_limit_bytes=2**20
        ),
    )(fields)


def body(fields, ocean_mask, gain_one, w_qkv, rel_bias, w_proj, gain_two, w_up, w_down):
    lat_cells, lon_cells, levels, features = fields.shape
    lat_windows = lat_cells // WIN_LAT
    lon_windows = lon_cells // WIN_LON
    slots = (lat_windows - 1) * lon_windows // 2
    north, east, corner = exchange_halos(fields)
    heads, length = rel_bias.shape
    group = WIN_LON * levels
    where = jnp.reshape(lax.axis_index("lon"), (1,)).astype(jnp.int32)
    shape = (WIN_LAT, WIN_LON, levels, features)
    window_count = lat_windows * lon_windows
    own, leaving, info, strips = pl.pallas_call(
        functools.partial(gather_kernel, slots),
        out_shape=[
            jax.ShapeDtypeStruct((slots,) + shape, fields.dtype),
            jax.ShapeDtypeStruct((slots,) + shape, fields.dtype),
            jax.ShapeDtypeStruct((2,), jnp.int32),
            jax.ShapeDtypeStruct((heads, group, 2 * WIN_LAT * group), jnp.float32),
        ],
        in_specs=[smem(), smem(), vmem()] + [any_space()] * 4,
        out_specs=[vmem(), vmem(), smem(), vmem()],
        scratch_shapes=[
            pltpu.VMEM((heads, (length + 255) // 128 * 128), jnp.float32),
            pltpu.SemaphoreType.DMA((window_count,)),
        ],
        cost_estimate=cost(0, 4 * fields.size),
        compiler_params=pltpu.CompilerParams(vmem_limit_bytes=6 * 2**20),
    )(ocean_mask, where, rel_bias, fields, north, east, corner)
    finished, returned = run_windows(
        info, own, leaving, strips, gain_one.reshape(1, -1), w_qkv, w_proj,
        gain_two.reshape(1, -1), w_up, w_down,
    )
    return pl.pallas_call(
        place_kernel,
        out_shape=jax.ShapeDtypeStruct(fields.shape, fields.dtype),
        in_specs=[smem()] * 3 + [any_space()] * 2,
        out_specs=any_space(),
        scratch_shapes=[
            pltpu.VMEM(shape, fields.dtype),
            pltpu.SemaphoreType.DMA((window_count,)),
        ],
        cost_estimate=cost(0, 4 * fields.size),
        compiler_params=pltpu.CompilerParams(vmem_limit_bytes=2**20),
    )(ocean_mask, where, info, finished, returned)


def solution(mesh):
    in_specs = (P("lat", "lon", None, None), P("lat", None), P(), P(), P(), P(), P(), P(), P())
    out_specs = P("lat", "lon", None, None)
    return jax.shard_map(body, mesh=mesh, in_specs=in_specs, out_specs=out_specs, check_vma=False)
```
